128 devices in a mesh: lat: 8 (over y_lo, z), lon: 16 (over x, y_hi, core).
Axes of the slice: x: 4, y: 4 (y_hi: 2, y_lo: 2; y = y_hi * 2 + y_lo), z: 4, core: 2. Of those that a mesh axis runs over, the one named last changes fastest.
Arguments:
- state: bfloat16 [64, 6144, 128], P('lat', 'lon'), may hold values from -6 to 6
- forcing: bfloat16 [64, 6144, 128], P('lat', 'lon'), may hold values from -4 to 4
- cotangent: bfloat16 [64, 6144, 128], P('lat', 'lon'), may hold values from -6 to 6
- land_mask: int32 [64, 6144], P('lat', 'lon'), may hold values 0 or 1
- dw_weight: bfloat16 [7, 7, 128], replicated, may hold values from -0.875 to 0.875
- dw_bias: float32 [128], replicated, may hold values from -3 to 3
- norm_gain: float32 [128], replicated, may hold values from 0.5 to 1.5
- norm_bias: float32 [128], replicated, may hold values from -3 to 3
- up_weight: bfloat16 [128, 512], replicated, may hold values from -0.5 to 0.5
- up_bias: float32 [512], replicated, may hold values from -3 to 3
- down_weight: bfloat16 [512, 128], replicated, may hold values from -0.25 to 0.25
- down_bias: float32 [128], replicated, may hold values from -3 to 3
- layer_scale: float32 [128], replicated, may hold values from 0.3 to 1
- owner: int32 [786432, 1], P(('lat', 'lon')), may hold values from 0 to 127; in each aligned block of 6144 rows (0 to 6143, 6144 to 12287, ...) at most 96 rows name the same one
- atmos_cell: int32 [786432], P(('lat', 'lon')), may hold values from 0 to 511
- weight_index: int32 [786432], P(('lat', 'lon')), may hold values from 0 to 15
- intersection_weights: float32 [16], replicated, may hold values from 0.1 to 1
Outputs:
- result: bfloat16 [64, 6144, 128], P('lat', 'lon')
- grad_dw: float32 [7, 7, 128], replicated
- grad_up: float32 [128, 512], replicated
- grad_down: float32 [512, 128], replicated
- forcing_grad: float32 [65536, 128], P(('lat', 'lon'))
The draws below stay inside these ranges and needn't reach their ends.
Inputs may be any that keep to these rules, and one draw needn't show every extreme that they name: At most 96 entries of one device name the same owner, and in every draw some device's entries name some owner exactly 96 times.
All inputs are finite; a program needn't handle non-finite values. No bound on the sum of `land_mask` on one device may be relied on, other than what follows from the above.
Results may differ from the reference program's by a relative error of at most 0.0071.
Values may be sent and summed in bfloat16 or wider, within the bound.
A program may use at most 128 MiB of HBM per device.

```python
import math
import jax
import jax.numpy as jnp
import numpy as np
from jax import lax

C = 128
HID = 512
KS = 7
NW = 16
CLAT = 8
CLON = 384
A_DEV = 512
NLAT = 64
NLON = 6144
ENT_DEV = 6144
ENTRIES = 786432
ATMOS = 65536
CAP = 96
N_LAT = 8
N_LON = 16
DEVICES = 128


def touch_ends(array, stream_key, low, high):
    longest = array.shape.index(max(array.shape))
    spots = []
    for shift in (0, 1):
        where = [jax.random.randint(jax.random.fold_in(stream_key, axis), (), 0, length) for axis, length in enumerate(array.shape)]
        where[longest] = (where[longest] + shift) % array.shape[longest]
        spots.append(tuple(where))
    return array.at[spots[0]].set(low).at[spots[1]].set(high)


def block_levels(own_key, extent, split, low, largest):
    loudness = 1.0
    for axis_at, shards_of in split:
        heights = jax.random.uniform(jax.random.fold_in(jax.random.fold_in(own_key, 6), axis_at), (shards_of,), jnp.float32, low / len(split), largest / len(split))
        loudness = loudness * jnp.repeat(jnp.exp(heights), extent[axis_at] // shards_of).reshape((-1,) + (1,) * (len(extent) - 1 - axis_at))
    return loudness


def shared_out(key, own, number, rows, count, top, bound, skew):
    order = jax.random.permutation(key, count)
    packed, ordinary = load_shares(count, rows * top, bound, skew, True), load_shares(count, rows * top, bound, skew, False)
    places = jnp.arange(count)

    def named(tallies, offset_by):
        used = int((tallies > 0).sum())
        fixed = max(1, used // 4)
        passed = fixed + (places - fixed + offset_by * (used - fixed)) % max(1, count - fixed)
        return jnp.zeros((count,), jnp.int32).at[order[jnp.where(places < fixed, places, passed)]].set(jnp.asarray(tallies, jnp.int32))

    tallies = jnp.where(number % 4 == 0, named(packed, number // 4), named(ordinary, number - number // 4 - 1))
    mixed = jax.random.permutation(jax.random.fold_in(own, 3), count)
    donor, receiver = mixed[0:count // 2 * 2:2], mixed[1:count // 2 * 2:2]
    slack = jnp.minimum(tallies[donor] - 1, bound - tallies[receiver]) // 2
    slack = jnp.where((donor == order[0]) | (receiver == order[0]) | (tallies[receiver] == 0), 0, jnp.maximum(slack, 0))
    passed = jax.random.randint(jax.random.fold_in(own, 4), (count // 2,), 0, 1 << 20) % (slack + 1)
    tallies = tallies.at[donor].add(-passed).at[receiver].add(passed)
    items = jnp.searchsorted(jnp.cumsum(tallies), jnp.arange(rows * top), side="right").astype(jnp.int32)
    grid = items.reshape(top, rows).T
    grid = grid[jax.random.permutation(jax.random.fold_in(own, 1), rows)]
    offset_by = jax.random.randint(jax.random.fold_in(own, 2), (rows, 1), 0, top)
    return jnp.take_along_axis(grid, (jnp.arange(top)[None, :] + offset_by) % top, axis=1)


def load_shares(amount, total, limit, skew, full):
    portions = [(1 << 20) // math.isqrt(rank ** skew) + 1 for rank in range(1, amount + 1)]
    largest = limit if full else min(limit, max(-(-total // amount), total * portions[0] // sum(portions)))
    least = 1 if total - largest >= amount - 1 else 0
    counts, surplus = [largest] + [least] * (amount - 1), total - largest - least * (amount - 1)
    while surplus > 0:
        candidates = [i for i in range(1, amount) if counts[i] < largest] or [i for i in range(1, amount) if counts[i] < limit]
        whole, remaining = sum([portions[i] for i in candidates]), surplus
        for i in candidates:
            addition = min(limit - counts[i], max(1, remaining * portions[i] // whole), surplus)
            counts[i] = counts[i] + addition
            surplus = surplus - addition
    return np.array(counts)


def bell_draw(rng, extent, spread, bound, pieces=(), held_as=jnp.bfloat16):
    array = jax.random.normal(rng, extent, jnp.float32) * spread
    if len(pieces) > 0:
        array = block_levels(rng, extent, pieces, -0.22, 0.18) * array
    return jnp.clip(array, min=-bound, max=bound).astype(held_as)


def setup_inputs(seed: int = 0) -> dict:
    splits = jax.random.split(jax.random.key(seed), 18)
    state = bell_draw(splits[0], (NLAT, NLON, C), 1.0, 6.0, ((0, 8), (1, 16)))
    forcing = bell_draw(splits[1], (NLAT, NLON, C), 0.5, 4.0, ((0, 8), (1, 16)))
    cotangent = bell_draw(splits[2], (NLAT, NLON, C), 1.0, 6.0, ((0, 8), (1, 16)))
    land_mask = touch_ends((jax.random.randint(splits[3], (NLAT, NLON), 0, 10) < 7).astype(jnp.int32), jax.random.fold_in(splits[3], 1), 0, 1)
    dw_weight = bell_draw(splits[4], (KS, KS, C), (KS * KS) ** -0.5, 0.875)
    dw_bias = bell_draw(splits[5], (C,), 0.5, 3.0, (), jnp.float32)
    norm_gain = jnp.clip(jax.random.uniform(splits[6], (C,), jnp.float32, 0.5, 1.5), 0.5, 1.5)
    norm_bias = bell_draw(splits[7], (C,), 0.5, 3.0, (), jnp.float32)
    up_weight = bell_draw(splits[8], (C, HID), C ** -0.5, 0.5)
    up_bias = bell_draw(splits[9], (HID,), 0.5, 3.0, (), jnp.float32)
    down_weight = bell_draw(splits[10], (HID, C), HID ** -0.5, 0.25)
    down_bias = bell_draw(splits[11], (C,), 0.5, 3.0, (), jnp.float32)
    layer_scale = jnp.clip(jnp.exp(jax.random.uniform(splits[12], (C,), jnp.float32, math.log(0.3), math.log(1.0))), 0.3, 1.0)
    owner_keys = jax.random.split(jax.random.fold_in(splits[13], 1), ENTRIES // ENT_DEV)
    owner_turns = jax.random.permutation(jax.random.fold_in(splits[13], 3), ENTRIES // ENT_DEV)
    owner = jax.vmap(lambda own, number: shared_out(jax.random.fold_in(splits[13], 2), own, number, ENT_DEV, DEVICES, 1, CAP, 2))(owner_keys, owner_turns).reshape((ENTRIES, 1))
    atmos_cell = touch_ends(jax.random.randint(splits[14], (ENTRIES,), 0, A_DEV), jax.random.fold_in(splits[14], 1), 0, A_DEV - 1).astype(jnp.int32)
    weight_index = touch_ends(jax.random.randint(splits[15], (ENTRIES,), 0, NW), jax.random.fold_in(splits[15], 1), 0, NW - 1).astype(jnp.int32)
    intersection_weights = jnp.clip(jnp.exp(jax.random.uniform(splits[16], (NW,), jnp.float32, math.log(0.1), math.log(1.0))), 0.1, 1.0)
    return {"state": state, "forcing": forcing, "cotangent": cotangent, "land_mask": land_mask, "dw_weight": dw_weight, "dw_bias": dw_bias, "norm_gain": norm_gain, "norm_bias": norm_bias, "up_weight": up_weight, "up_bias": up_bias, "down_weight": down_weight, "down_bias": down_bias, "layer_scale": layer_scale, "owner": owner, "atmos_cell": atmos_cell, "weight_index": weight_index, "intersection_weights": intersection_weights}


gelu_scale = 0.7978845608028654
cubic_coef = 0.044715

def gelu_pair(pre):
    inner = gelu_scale * (pre + cubic_coef * pre * pre * pre)
    tanh_value = jnp.tanh(inner)
    value = 0.5 * pre * (1.0 + tanh_value)
    slope = 0.5 * (1.0 + tanh_value) + 0.5 * pre * (1.0 - tanh_value * tanh_value) * gelu_scale * (1.0 + 3.0 * cubic_coef * pre * pre)
    return (value, slope)

def depthwise(padded, kernel):
    channels = padded.shape[-1]
    convolved = lax.conv_general_dilated(padded[None], kernel[:, :, None, :], (1, 1), 'VALID', dimension_numbers=('NHWC', 'HWIO', 'NHWC'), feature_group_count=channels, preferred_element_type=jnp.float32)
    return convolved[0]

def block_pass(padded, state, forcing, cotangent, land, dw_weight, dw_bias, norm_gain, norm_bias, up_weight, up_bias, down_weight, down_bias, layer_scale):
    tile_rows, tile_cols, channels = state.shape
    conv = depthwise(padded, dw_weight) + dw_bias
    average = lax.optimization_barrier(jnp.mean(conv, axis=-1, keepdims=True))
    centred = conv - average
    variance = lax.optimization_barrier(jnp.mean(centred * centred, axis=-1, keepdims=True))
    inv_std = lax.rsqrt(variance + 1e-06)
    normed = centred * inv_std
    mixed = (normed * norm_gain + norm_bias + forcing.astype(jnp.float32)).astype(jnp.bfloat16)
    flat = mixed.reshape(-1, channels)
    pre = jnp.dot(flat, up_weight, preferred_element_type=jnp.float32) + up_bias
    activated, slope = gelu_pair(pre)
    hidden = activated.astype(jnp.bfloat16)
    projected = jnp.dot(hidden, down_weight, preferred_element_type=jnp.float32) + down_bias
    ocean = land.astype(jnp.float32).reshape(-1, 1)
    result = (ocean * (state.reshape(-1, channels).astype(jnp.float32) + layer_scale * projected)).astype(jnp.bfloat16)
    grad_out = (ocean * layer_scale * cotangent.reshape(-1, channels).astype(jnp.float32)).astype(jnp.bfloat16)
    down_term = jnp.dot(hidden.T, grad_out, preferred_element_type=jnp.float32)
    grad_hidden = jnp.dot(grad_out, down_weight.T, preferred_element_type=jnp.float32)
    grad_pre = (grad_hidden * slope).astype(jnp.bfloat16)
    up_term = jnp.dot(flat.T, grad_pre, preferred_element_type=jnp.float32)
    grad_mixed = jnp.dot(grad_pre, up_weight.T, preferred_element_type=jnp.float32).reshape(tile_rows, tile_cols, channels)
    gained = grad_mixed * norm_gain
    grad_conv = (inv_std * (gained - lax.optimization_barrier(jnp.mean(gained, axis=-1, keepdims=True)) - normed * lax.optimization_barrier(jnp.mean(gained * normed, axis=-1, keepdims=True)))).astype(jnp.bfloat16)
    conv_term = depthwise(padded, grad_conv)
    return (result.reshape(tile_rows, tile_cols, channels), grad_mixed, conv_term, up_term, down_term)

def pad_grid(state, margin):
    lon_padded = jnp.concatenate([state[:, -margin:], state, state[:, :margin]], axis=1)
    below = jnp.zeros((margin,) + lon_padded.shape[1:], state.dtype)
    above = lon_padded[-margin:][::-1, ::-1]
    return jnp.concatenate([below, lon_padded, above], axis=0)

def reference(state, forcing, cotangent, land_mask, dw_weight, dw_bias, norm_gain, norm_bias, up_weight, up_bias, down_weight, down_bias, layer_scale, owner, atmos_cell, weight_index, intersection_weights):
    margin = KS // 2
    padded = pad_grid(state, margin)
    band_rows = 4
    band_count = NLAT // band_rows

    def band_step(totals, block_id):
        start = block_id * band_rows
        pad_rows = lax.dynamic_slice_in_dim(padded, start, band_rows + 2 * margin, 0)
        state_rows = lax.dynamic_slice_in_dim(state, start, band_rows, 0)
        forcing_rows = lax.dynamic_slice_in_dim(forcing, start, band_rows, 0)
        cot_rows = lax.dynamic_slice_in_dim(cotangent, start, band_rows, 0)
        land_rows = lax.dynamic_slice_in_dim(land_mask, start, band_rows, 0)
        result, grad_mixed, conv_term, up_term, down_term = block_pass(pad_rows, state_rows, forcing_rows, cot_rows, land_rows, dw_weight, dw_bias, norm_gain, norm_bias, up_weight, up_bias, down_weight, down_bias, layer_scale)
        return ((totals[0] + conv_term, totals[1] + up_term, totals[2] + down_term), (result, grad_mixed))
    zeros_init = (jnp.zeros((KS, KS, C), jnp.float32), jnp.zeros((C, HID), jnp.float32), jnp.zeros((HID, C), jnp.float32))
    totals, (results, grad_bands) = lax.scan(band_step, zeros_init, jnp.arange(band_count, dtype=jnp.int32))
    scale = float(NLAT * NLON) ** (-0.5)
    grad_dw = totals[0] * scale
    grad_up = totals[1] * scale
    grad_down = totals[2] * scale
    result = results.reshape(NLAT, NLON, C)
    tiles = grad_bands.reshape(N_LAT, CLAT, N_LON, CLON, C)
    table_hit = weight_index[:, None] == jnp.arange(NW, dtype=jnp.int32)[None, :]
    entry_weights = lax.optimization_barrier(jnp.sum(jnp.where(table_hit, intersection_weights[None, :], 0.0), axis=1))
    owners = owner[:, 0]

    def regrid_step(total, device_id):
        band = lax.dynamic_index_in_dim(tiles, device_id // N_LON, 0, keepdims=False)
        device_tile = lax.dynamic_index_in_dim(band, device_id % N_LON, 1, keepdims=False)
        per_entry = jnp.repeat(device_tile.reshape(CLAT * CLON, C), 2, axis=0)
        offset = device_id * ENT_DEV
        weights_here = lax.dynamic_slice_in_dim(entry_weights, offset, ENT_DEV)
        rounded = (weights_here[:, None] * per_entry).astype(jnp.bfloat16)
        rounded = lax.optimization_barrier(rounded).astype(jnp.float32)
        targets = lax.dynamic_slice_in_dim(owners, offset, ENT_DEV) * A_DEV + lax.dynamic_slice_in_dim(atmos_cell, offset, ENT_DEV)
        return (total.at[targets].add(rounded), None)
    forcing_grad, _ = lax.scan(regrid_step, jnp.zeros((ATMOS, C), jnp.float32), jnp.arange(DEVICES, dtype=jnp.int32))
    return (result, grad_dw, grad_up, grad_down, forcing_grad)
```

```python
import functools

import jax
import jax.numpy as jnp
from jax import lax
from jax.experimental import pallas as pl
from jax.experimental.pallas import tpu as pltpu
from jax.sharding import PartitionSpec as P

F32 = jnp.float32
BF16 = jnp.bfloat16
I32 = jnp.int32
MESH = pl.DeviceIdType.MESH
VMEM_SPEC = pl.BlockSpec(memory_space=pltpu.VMEM)
SMEM_SPEC = pl.BlockSpec(memory_space=pltpu.SMEM)
ANY_SPEC = pl.BlockSpec(memory_space=pl.ANY)

A_DEV = 512
LANES = 128
CAP = 96
MARGIN = 3
TAPS = 7
LAT = 8
LON = 16
DEVICES = LAT * LON
PART_ROWS = 144

gelu_scale = 0.7978845608028654
cubic_coef = 0.044715


def nt_dot(a, b):
    return lax.dot_general(a, b, (((1,), (1,)), ((), ())), preferred_element_type=F32)


def nn_dot(a, b):
    return jnp.dot(a, b, preferred_element_type=F32)


def rank_kernel(owner_ref, cell_ref, index_ref, table_ref, slot_ref, weight_ref, cells_ref, base, acc):
    blocks = owner_ref.shape[0]
    group = 8
    base[...] = jnp.zeros_like(base)
    acc[...] = jnp.zeros_like(acc)
    row_id = lax.broadcasted_iota(I32, (LANES, LANES), 0)
    col_id = lax.broadcasted_iota(I32, (LANES, LANES), 1)
    tri = jnp.concatenate(
        [jnp.where(row_id < col_id, 1.0, 0.0), jnp.ones((LANES, LANES), F32)], axis=1
    ).astype(BF16)

    index = index_ref[...]
    weight = jnp.zeros(index.shape, F32)
    for entry in range(table_ref.shape[0]):
        weight = jnp.where(index == entry, table_ref[entry], weight)
    weight_ref[...] = weight

    def body(step, carry):
        start = pl.multiple_of(step * group, group)
        owners = owner_ref[pl.ds(start, group), :]
        coded = cell_ref[pl.ds(start, group), :] + 1
        high = (coded >> 1).astype(F32)
        low = (coded & 1).astype(F32)
        ranks = []
        for i in range(group):
            hit = row_id == owners[i : i + 1, :]
            hot = jnp.where(hit, 1.0, 0.0)
            hot16 = hot.astype(BF16)
            sums = nn_dot(hot16, tri)
            before = sums[:, :LANES] + base[...]
            rank = jnp.sum(hot * before, axis=0, keepdims=True)
            ranks.append(rank)
            base[...] += sums[:, LANES:]
            at_rank = row_id == rank.astype(I32)
            spread = jnp.concatenate(
                [
                    jnp.where(at_rank, high[i : i + 1, :], 0.0),
                    jnp.where(at_rank, low[i : i + 1, :], 0.0),
                ],
                axis=0,
            ).astype(BF16)
            acc[...] += nt_dot(hot16, spread)
        rank8 = jnp.concatenate(ranks, axis=0).astype(I32)
        slot_ref[pl.ds(start, group), :] = owners * CAP + rank8
        return carry

    lax.fori_loop(0, blocks // group, body, 0)
    total = acc[...]
    cells_ref[...] = (2.0 * total[:, :LANES] + total[:, LANES:]).astype(I32) - 1


def rank_entries(owner, atmos_cell, weight_index, table):
    entries = owner.shape[0]
    shape = (entries // LANES, LANES)
    return pl.pallas_call(
        rank_kernel,
        out_shape=(
            jax.ShapeDtypeStruct(shape, I32),
            jax.ShapeDtypeStruct(shape, F32),
            jax.ShapeDtypeStruct((DEVICES, LANES), I32),
        ),
        in_specs=[VMEM_SPEC, VMEM_SPEC, VMEM_SPEC, SMEM_SPEC],
        out_specs=[VMEM_SPEC, VMEM_SPEC, VMEM_SPEC],
        scratch_shapes=[pltpu.VMEM((LANES, LANES), F32), pltpu.VMEM((LANES, 2 * LANES), F32)],
        name="rank_entries",
        cost_estimate=pl.CostEstimate(flops=10**9, bytes_accessed=10**6, transcendentals=0),
    )(owner.reshape(shape), atmos_cell.reshape(shape), weight_index.reshape(shape), table)


def block_kernel(
    padded_ref,
    state_ref,
    forcing_ref,
    cot_ref,
    land_ref,
    dw_ref,
    chan_ref,
    up_ref,
    up_bias_ref,
    down_ref,
    slot_ref,
    weight_ref,
    result_ref,
    parts_ref,
    send_ref,
    xf,
    wts,
    conv,
    gconv,
    gm,
    pre,
    gh,
    hid,
    gp,
    norm,
    up_acc,
    down_acc,
    buf,
):
    rows, cols, channels = state_ref.shape
    hidden_units = up_ref.shape[1]
    dw_bias = chan_ref[0:1, :]
    gain = chan_ref[1:2, :]
    shift = chan_ref[2:3, :]
    down_bias = chan_ref[3:4, :]
    scale = chan_ref[4:5, :]

    def zero_body(i, carry):
        buf[pl.ds(pl.multiple_of(i * 128, 128), 128), :] = jnp.zeros((128, channels), F32)
        return carry

    lax.fori_loop(0, buf.shape[0] // 128, zero_body, 0)
    up_acc[...] = jnp.zeros_like(up_acc)
    down_acc[...] = jnp.zeros_like(down_acc)

    def unpack(i, carry):
        xf[i] = padded_ref[i].astype(F32)
        return carry

    lax.fori_loop(0, rows + 2 * MARGIN, unpack, 0)
    for tap in range(TAPS * TAPS):
        wts[tap] = jnp.broadcast_to(dw_ref[tap : tap + 1, :], (8, channels))

    def conv_body(block, carry):
        start = block * 8
        total = [jnp.broadcast_to(dw_bias, (8, channels)) for _ in range(rows)]
        for b in range(TAPS):
            xs = [xf[line, pl.ds(start + b, 8), :] for line in range(rows + TAPS - 1)]
            for a in range(TAPS):
                wv = wts[a * TAPS + b]
                for r in range(rows):
                    total[r] = total[r] + xs[r + a] * wv
        for r in range(rows):
            conv[r, pl.ds(pl.multiple_of(start, 8), 8), :] = total[r]
        return carry

    lax.fori_loop(0, cols // 8, conv_body, 0)

    land = land_ref[...].astype(F32)
    line_id = lax.broadcasted_iota(I32, land.shape, 0)
    ones = jnp.ones((rows, channels), BF16)

    def tile_body(r, carry):
        field = conv[r]
        centred = field - jnp.mean(field, axis=-1, keepdims=True)
        inv_std = lax.rsqrt(jnp.mean(centred * centred, axis=-1, keepdims=True) + 1e-06)
        normed = centred * inv_std
        norm[...] = normed
        mixed = (normed * gain + shift + forcing_ref[r].astype(F32)).astype(BF16)
        own_line = jnp.where(line_id == r, land, 0.0).astype(BF16)
        ocean = lax.dot_general(
            own_line, ones, (((0,), (0,)), ((), ())), preferred_element_type=F32
        )
        grad_out = (ocean * scale * cot_ref[r].astype(F32)).astype(BF16)
        pre[...] = nn_dot(mixed, up_ref[...]) + up_bias_ref[...]
        gh[...] = nt_dot(grad_out, down_ref[...])

        def gelu_body(i, carry):
            start = pl.multiple_of(i * 16, 16)
            p = pre[pl.ds(start, 16), :]
            u = p * p
            half = 0.5 + 0.5 * jnp.tanh(p * (gelu_scale + gelu_scale * cubic_coef * u))
            value = p * half
            slope = half + value * (1.0 - half) * (
                2.0 * gelu_scale + 6.0 * gelu_scale * cubic_coef * u
            )
            hid[pl.ds(start, 16), :] = value.astype(BF16)
            gp[pl.ds(start, 16), :] = (gh[pl.ds(start, 16), :] * slope).astype(BF16)
            return carry

        lax.fori_loop(0, cols // 16, gelu_body, 0)
        hidden = hid[...]
        grad_pre = gp[...]
        projected = nn_dot(hidden, down_ref[...]) + down_bias
        result_ref[r] = (ocean * (state_ref[r].astype(F32) + scale * projected)).astype(BF16)
        down_acc[...] += nn_dot(grad_out.T, hidden)
        up_acc[...] += nn_dot(mixed.T, grad_pre)
        grad_mixed = nt_dot(grad_pre, up_ref[...])
        gm[pl.ds(pl.multiple_of(r * cols, cols), cols), :] = grad_mixed
        gained = grad_mixed * gain
        normed2 = norm[...]
        back = (
            gained
            - jnp.mean(gained, axis=-1, keepdims=True)
            - normed2 * jnp.mean(gained * normed2, axis=-1, keepdims=True)
        ) * inv_std
        gconv[r] = back.astype(BF16).astype(F32)
        return carry

    lax.fori_loop(0, rows, tile_body, 0)

    unit = 8

    def pack_body(i, carry):
        first = i * unit
        for k in range(unit):
            line = gm[pl.ds(first + k, 1), :]
            for j in range(2):
                entry = 2 * first + 2 * k + j
                buf[pl.ds(slot_ref[entry], 1), :] = line * weight_ref[entry]
        return carry

    lax.fori_loop(0, rows * cols // unit, pack_body, 0)

    for blk in range(hidden_units // LANES):
        parts_ref[blk, 0:LANES, :] = up_acc[:, blk * LANES : (blk + 1) * LANES].astype(BF16)
        parts_ref[4 + blk, 0:LANES, :] = down_acc[:, blk * LANES : (blk + 1) * LANES].T.astype(BF16)
    parts_ref[TAPS, LANES:, :] = jnp.zeros((PART_ROWS - LANES, channels), BF16)

    sums = [[None] * TAPS for _ in range(TAPS)]
    for b in range(TAPS):

        def corr_body(block, carry):
            start = block * 8
            xs = [xf[line, pl.ds(start + b, 8), :] for line in range(rows + TAPS - 1)]
            gs = [gconv[r, pl.ds(pl.multiple_of(start, 8), 8), :] for r in range(rows)]
            out = []
            for a in range(TAPS):
                total = carry[a]
                for r in range(rows):
                    total = total + xs[r + a] * gs[r]
                out.append(total)
            return tuple(out)

        done = lax.fori_loop(
            0, cols // 8, corr_body, tuple(jnp.zeros((8, channels), F32) for _ in range(TAPS))
        )
        for a in range(TAPS):
            sums[a][b] = jnp.sum(done[a], axis=0, keepdims=True)
    for a in range(TAPS):
        lines = sums[a] + [jnp.zeros((PART_ROWS - LANES - TAPS, channels), F32)]
        parts_ref[a, LANES:, :] = jnp.concatenate(lines, axis=0).astype(BF16)

    def cast_body(i, carry):
        send_ref[i] = buf[pl.ds(pl.multiple_of(i * CAP, CAP), CAP), :].astype(BF16)
        return carry

    lax.fori_loop(0, DEVICES, cast_body, 0)


def run_block(padded, state, forcing, cotangent, land, dw, chan, up, up_bias, down, slots, weights):
    rows, cols, channels = state.shape
    hidden = up.shape[1]
    wide = padded.shape[1]
    lines = padded.shape[0]
    return pl.pallas_call(
        block_kernel,
        out_shape=(
            jax.ShapeDtypeStruct(state.shape, BF16),
            jax.ShapeDtypeStruct((LAT, PART_ROWS, LANES), BF16),
            jax.ShapeDtypeStruct((DEVICES, CAP, channels), BF16),
        ),
        in_specs=[VMEM_SPEC] * 10 + [SMEM_SPEC] * 2,
        out_specs=[VMEM_SPEC] * 3,
        scratch_shapes=[
            pltpu.VMEM((lines, wide, channels), F32),
            pltpu.VMEM((TAPS * TAPS, 8, channels), F32),
            pltpu.VMEM((rows, cols, channels), F32),
            pltpu.VMEM((rows, cols, channels), F32),
            pltpu.VMEM((rows * cols, channels), F32),
            pltpu.VMEM((cols, hidden), F32),
            pltpu.VMEM((cols, hidden), F32),
            pltpu.VMEM((cols, hidden), BF16),
            pltpu.VMEM((cols, hidden), BF16),
            pltpu.VMEM((cols, channels), F32),
            pltpu.VMEM((channels, hidden), F32),
            pltpu.VMEM((channels, hidden), F32),
            pltpu.VMEM((DEVICES * CAP, channels), F32),
        ],
        name="block_pass",
        cost_estimate=pl.CostEstimate(
            flops=3 * 10**9, bytes_accessed=10**7, transcendentals=rows * cols * hidden
        ),
    )(padded, state, forcing, cotangent, land, dw, chan, up, up_bias, down, slots, weights)


def exchange_kernel(
    factor,
    rows_hbm,
    cells_hbm,
    parts_ref,
    up_ref,
    down_ref,
    dw_ref,
    grad_ref,
    recv_rows,
    recv_cells,
    recv1,
    send2,
    recv2,
    send3,
    recv3,
    send4,
    recv4,
    row_send,
    row_recv,
    cell_send,
    cell_recv,
    send_sem,
    recv_sem,
):
    lat = lax.axis_index("lat")
    lon = lax.axis_index("lon")
    me = lat * LON + lon

    def device(k):
        peer = lax.rem(me + k, DEVICES)
        return (peer // LON, lax.rem(peer, LON))

    barrier = pltpu.get_barrier_semaphore()

    def greet(k, carry):
        pl.semaphore_signal(barrier, inc=1, device_id=device(k), device_id_type=MESH)
        return carry

    lax.fori_loop(1, DEVICES, greet, 0)

    recv_rows[:, CAP:, :] = jnp.zeros((DEVICES, LANES - CAP, LANES), BF16)
    grad_ref[...] = jnp.zeros_like(grad_ref)
    pl.semaphore_wait(barrier, DEVICES - 1)

    def row_copy(k):
        to = device(k)
        peer = to[0] * LON + to[1]
        return (
            pltpu.make_async_remote_copy(
                src_ref=rows_hbm.at[peer],
                dst_ref=recv_rows.at[k, pl.ds(0, CAP)],
                send_sem=row_send.at[k],
                recv_sem=row_recv.at[k],
                device_id=to,
                device_id_type=MESH,
            ),
            pltpu.make_async_remote_copy(
                src_ref=cells_hbm.at[peer],
                dst_ref=recv_cells.at[k],
                send_sem=cell_send.at[k],
                recv_sem=cell_recv.at[k],
                device_id=to,
                device_id_type=MESH,
            ),
        )

    def send_range(first, last):
        def body(k, carry):
            for copy in row_copy(k):
                copy.start()
            return carry

        lax.fori_loop(first, last, body, 0)

    own_rows = pltpu.make_async_copy(rows_hbm.at[me], recv_rows.at[0, pl.ds(0, CAP)], row_recv.at[0])
    own_cells = pltpu.make_async_copy(cells_hbm.at[me], recv_cells.at[0], cell_recv.at[0])

    def lat_copy(stage, k, src, dst):
        to = lax.rem(lat + k, LAT)
        return pltpu.make_async_remote_copy(
            src_ref=src(to),
            dst_ref=dst.at[k],
            send_sem=send_sem.at[stage, k],
            recv_sem=recv_sem.at[stage, k],
            device_id=(to, lon),
            device_id_type=MESH,
        )

    def lon_copy(stage, k, src, dst):
        to = lax.rem(lon + k, LON)
        return pltpu.make_async_remote_copy(
            src_ref=src(to),
            dst_ref=dst.at[k],
            send_sem=send_sem.at[stage, k],
            recv_sem=recv_sem.at[stage, k],
            device_id=(lat, to),
            device_id_type=MESH,
        )

    def copy1(k):
        return lat_copy(0, k, lambda to: parts_ref.at[to], recv1)

    def copy2(k):
        return lon_copy(1, k, lambda to: send2.at[to], recv2)

    def copy3(k):
        return lon_copy(2, k, lambda to: send3, recv3)

    def copy4(k):
        return lat_copy(3, k, lambda to: send4, recv4)

    def start_all(copy, count):
        def body(k, carry):
            copy(k).start()
            return carry

        lax.fori_loop(1, count, body, 0)

    def arrive_all(copy, count):
        def body(k, carry):
            copy(k).wait_recv()
            return carry

        lax.fori_loop(1, count, body, 0)

    def left_all(copy, count):
        def body(k, carry):
            copy(k).wait_send()
            return carry

        lax.fori_loop(1, count, body, 0)

    start_all(copy1, LAT)
    own_rows.start()
    own_cells.start()
    send_range(1, 32)
    arrive_all(copy1, LAT)
    total = parts_ref[lat].astype(F32)
    for k in range(1, LAT):
        total = total + recv1[k].astype(F32)
    tail = total[LANES : LANES + 8, :]
    for j in range(LON):
        send2[j] = jnp.concatenate([total[8 * j : 8 * j + 8, :], tail], axis=0).astype(BF16)

    start_all(copy2, LON)
    send_range(32, 64)
    arrive_all(copy2, LON)
    total = send2[lon].astype(F32)
    for k in range(1, LON):
        total = total + recv2[k].astype(F32)
    send3[...] = total[:8, :]
    send4[LANES:, :] = jnp.concatenate([total[8:, :], jnp.zeros((8, LANES), F32)], axis=0).astype(BF16)

    start_all(copy3, LON)
    send_range(64, 96)
    arrive_all(copy3, LON)
    recv3[0] = send3[...]
    for j in range(LON // 2):
        pair = [recv3[lax.rem(lon - (2 * j + i) + LON, LON)] for i in range(2)]
        send4[16 * j : 16 * j + 16, :] = jnp.concatenate(pair, axis=0).astype(BF16)

    start_all(copy4, LAT)
    send_range(96, DEVICES)

    cell_id = lax.broadcasted_iota(I32, (A_DEV, LANES), 0)

    def add_pair(i):
        hot = jnp.concatenate(
            [jnp.where(cell_id == recv_cells[2 * i + j], 1.0, 0.0).astype(BF16) for j in range(2)],
            axis=1,
        )
        values = recv_rows[pl.ds(2 * i, 2)].reshape(2 * LANES, LANES)
        grad_ref[...] += nn_dot(hot, values)

    def wait_rows(k):
        for copy in row_copy(k):
            copy.wait_recv()

    own_rows.wait()
    own_cells.wait()
    wait_rows(1)
    add_pair(0)

    def pair_body(i, carry):
        wait_rows(2 * i)
        wait_rows(2 * i + 1)
        add_pair(i)
        return carry

    lax.fori_loop(1, DEVICES // 2, pair_body, 0)

    arrive_all(copy4, LAT)
    recv4[0] = send4[...]
    for chunk in range(LAT):
        block = recv4[lax.rem(lat - chunk + LAT, LAT)].astype(F32) * factor
        if chunk < 4:
            up_ref[:, chunk * LANES : (chunk + 1) * LANES] = block[:LANES]
        else:
            down_ref[(chunk - 4) * LANES : (chunk - 3) * LANES, :] = block[:LANES]
        if chunk < TAPS:
            dw_ref[chunk] = block[LANES : LANES + TAPS]

    left_all(copy1, LAT)
    left_all(copy2, LON)
    left_all(copy3, LON)
    left_all(copy4, LAT)

    def left_body(k, carry):
        for copy in row_copy(k):
            copy.wait_send()
        return carry

    lax.fori_loop(1, DEVICES, left_body, 0)


def exchange(rows, cells, parts, factor):
    dma = pltpu.SemaphoreType.DMA
    return pl.pallas_call(
        functools.partial(exchange_kernel, factor),
        out_shape=(
            jax.ShapeDtypeStruct((LANES, 512), F32),
            jax.ShapeDtypeStruct((512, LANES), F32),
            jax.ShapeDtypeStruct((TAPS, TAPS, LANES), F32),
            jax.ShapeDtypeStruct((A_DEV, LANES), F32),
        ),
        in_specs=[ANY_SPEC, ANY_SPEC, VMEM_SPEC],
        out_specs=[VMEM_SPEC] * 4,
        scratch_shapes=[
            pltpu.VMEM((DEVICES, LANES, LANES), BF16),
            pltpu.VMEM((DEVICES, 1, LANES), I32),
            pltpu.VMEM((LAT, PART_ROWS, LANES), BF16),
            pltpu.VMEM((LON, 16, LANES), BF16),
            pltpu.VMEM((LON, 16, LANES), BF16),
            pltpu.VMEM((8, LANES), F32),
            pltpu.VMEM((LON, 8, LANES), F32),
            pltpu.VMEM((PART_ROWS, LANES), BF16),
            pltpu.VMEM((LAT, PART_ROWS, LANES), BF16),
            dma((DEVICES,)),
            dma((DEVICES,)),
            dma((DEVICES,)),
            dma((DEVICES,)),
            dma((4, LON)),
            dma((4, LON)),
        ],
        compiler_params=pltpu.CompilerParams(collective_id=0, has_side_effects=True),
        name="exchange",
    )(rows, cells.reshape(DEVICES, 1, LANES), parts)


def extended(block, sides, width, periodic):
    for axis, dim in sides:
        count = lax.axis_size(axis)
        forward = [(i, i + 1) for i in range(count - 1)]
        if periodic:
            forward.append((count - 1, 0))
        backward = [(target, source) for source, target in forward]
        low = lax.ppermute(
            lax.slice_in_dim(block, block.shape[dim] - width, None, axis=dim), axis, forward
        )
        high = lax.ppermute(lax.slice_in_dim(block, 0, width, axis=dim), axis, backward)
        block = jnp.concatenate([low, block, high], axis=dim)
    return block


def on_device(
    state,
    forcing,
    cotangent,
    land_mask,
    dw_weight,
    dw_bias,
    norm_gain,
    norm_bias,
    up_weight,
    up_bias,
    down_weight,
    down_bias,
    layer_scale,
    owner,
    atmos_cell,
    weight_index,
    intersection_weights,
):
    rows, cols, channels = state.shape
    slots, weights, cells = rank_entries(owner[:, 0], atmos_cell, weight_index, intersection_weights)

    lon_ext = extended(state, (("lon", 1),), MARGIN, True)
    padded = extended(lon_ext, (("lat", 0),), MARGIN, False)
    partner = lax.ppermute(
        lon_ext[rows - MARGIN :], "lon", [(i, LON - 1 - i) for i in range(LON)]
    )
    mirrored = partner[::-1, ::-1]
    northmost = lax.axis_index("lat") == LAT - 1
    north_rows = jnp.where(northmost, mirrored, padded[rows + MARGIN :])
    padded = jnp.concatenate([padded[: rows + MARGIN], north_rows], axis=0)
    padded = jnp.pad(padded, ((0, 0), (0, 2), (0, 0)))

    chan = jnp.stack(
        [dw_bias, norm_gain, norm_bias, down_bias, layer_scale] + [jnp.zeros_like(dw_bias)] * 3
    )
    result, parts, send_rows = run_block(
        padded,
        state,
        forcing,
        cotangent,
        land_mask,
        dw_weight.astype(F32).reshape(TAPS * TAPS, channels),
        chan,
        up_weight,
        up_bias.reshape(1, -1),
        down_weight,
        slots.reshape(-1),
        weights.reshape(-1),
    )
    factor = float(rows * LAT * cols * LON) ** (-0.5)
    grad_up, grad_down, grad_dw, forcing_grad = exchange(send_rows, cells, parts, factor)
    return (result, grad_dw, grad_up, grad_down, forcing_grad)


def solution(mesh):
    in_specs = (
        P("lat", "lon", None),
        P("lat", "lon", None),
        P("lat", "lon", None),
        P("lat", "lon"),
        P(),
        P(),
        P(),
        P(),
        P(),
        P(),
        P(),
        P(),
        P(),
        P(("lat", "lon"), None),
        P(("lat", "lon")),
        P(("lat", "lon")),
        P(),
    )
    out_specs = (P("lat", "lon", None), P(), P(), P(), P(("lat", "lon"), None))
    return jax.shard_map(
        on_device, mesh=mesh, in_specs=in_specs, out_specs=out_specs, check_vma=False
    )
```

```python
import functools

import jax
import jax.numpy as jnp
from jax import lax
from jax.experimental import pallas as pl
from jax.experimental.pallas import tpu as pltpu
from jax.sharding import PartitionSpec as P

F32 = jnp.float32
BF16 = jnp.bfloat16
I32 = jnp.int32
MESH = pl.DeviceIdType.MESH
VMEM_SPEC = pl.BlockSpec(memory_space=pltpu.VMEM)
SMEM_SPEC = pl.BlockSpec(memory_space=pltpu.SMEM)
ANY_SPEC = pl.BlockSpec(memory_space=pl.ANY)

A_DEV = 512
LANES = 128
CAP = 96
MARGIN = 3
TAPS = 7
LAT = 8
LON = 16
DEVICES = LAT * LON
PART_ROWS = 144
STRIDE = 77
DW_ROWS = 16
CODE_BITS = 9

gelu_scale = 0.7978845608028654
cubic_coef = 0.044715


def nt_dot(a, b):
    return lax.dot_general(a, b, (((1,), (1,)), ((), ())), preferred_element_type=F32)


def nn_dot(a, b):
    return jnp.dot(a, b, preferred_element_type=F32)


def rank_kernel(owner_ref, cell_ref, index_ref, slot_ref, cells_ref, base, acc):
    blocks = owner_ref.shape[0]
    group = 8
    base[...] = jnp.zeros_like(base)
    acc[...] = jnp.zeros_like(acc)
    row_id = lax.broadcasted_iota(I32, (LANES, LANES), 0)
    col_id = lax.broadcasted_iota(I32, (LANES, LANES), 1)
    tri = jnp.concatenate(
        [jnp.where(row_id < col_id, 1.0, 0.0), jnp.ones((LANES, LANES), F32)], axis=1
    ).astype(BF16)

    def body(step, carry):
        start = pl.multiple_of(step * group, group)
        owners = owner_ref[pl.ds(start, group), :]
        coded = cell_ref[pl.ds(start, group), :] + (index_ref[pl.ds(start, group), :] << CODE_BITS) + 1
        high = (coded >> 7).astype(F32)
        low = (coded & 127).astype(F32)
        ranks = []
        for i in range(group):
            hit = row_id == owners[i : i + 1, :]
            hot = jnp.where(hit, 1.0, 0.0)
            hot16 = hot.astype(BF16)
            sums = nn_dot(hot16, tri)
            before = sums[:, :LANES] + base[...]
            rank = jnp.sum(hot * before, axis=0, keepdims=True)
            ranks.append(rank)
            base[...] += sums[:, LANES:]
            at_rank = row_id == rank.astype(I32)
            spread = jnp.concatenate(
                [
                    jnp.where(at_rank, high[i : i + 1, :], 0.0),
                    jnp.where(at_rank, low[i : i + 1, :], 0.0),
                ],
                axis=0,
            ).astype(BF16)
            acc[...] += nt_dot(hot16, spread)
        rank8 = jnp.concatenate(ranks, axis=0).astype(I32)
        slot_ref[pl.ds(start, group), :] = owners * CAP + rank8
        return carry

    lax.fori_loop(0, blocks // group, body, 0)
    total = acc[...]
    cells_ref[...] = (128.0 * total[:, :LANES] + total[:, LANES:]).astype(I32) - 1


def rank_entries(owner, atmos_cell, weight_index):
    entries = owner.shape[0]
    shape = (entries // LANES, LANES)
    return pl.pallas_call(
        rank_kernel,
        out_shape=(
            jax.ShapeDtypeStruct(shape, I32),
            jax.ShapeDtypeStruct((DEVICES, LANES), I32),
        ),
        in_specs=[VMEM_SPEC, VMEM_SPEC, VMEM_SPEC],
        out_specs=[VMEM_SPEC, VMEM_SPEC],
        scratch_shapes=[pltpu.VMEM((LANES, LANES), F32), pltpu.VMEM((LANES, 2 * LANES), F32)],
        name="rank_entries",
        cost_estimate=pl.CostEstimate(flops=10**9, bytes_accessed=10**6, transcendentals=0),
    )(owner.reshape(shape), atmos_cell.reshape(shape), weight_index.reshape(shape))


def block_kernel(
    padded_ref,
    state_ref,
    forcing_ref,
    cot_ref,
    land_ref,
    dw_ref,
    chan_ref,
    up_ref,
    up_bias_ref,
    down_ref,
    slot_ref,
    result_ref,
    parts_ref,
    send_ref,
    gconv_ref,
    xf,
    wts,
    conv,
    gm,
    pre,
    gh,
    hid,
    gp,
    norm,
    up_acc,
    down_acc,
    buf,
):
    rows, cols, channels = state_ref.shape
    hidden_units = up_ref.shape[1]
    dw_bias = chan_ref[0:1, :]
    gain = chan_ref[1:2, :]
    shift = chan_ref[2:3, :]
    down_bias = chan_ref[3:4, :]
    scale = chan_ref[4:5, :]

    def zero_body(i, carry):
        buf[pl.ds(pl.multiple_of(i * 128, 128), 128), :] = jnp.zeros((128, channels), F32)
        return carry

    lax.fori_loop(0, buf.shape[0] // 128, zero_body, 0)
    up_acc[...] = jnp.zeros_like(up_acc)
    down_acc[...] = jnp.zeros_like(down_acc)

    def unpack(i, carry):
        xf[i] = padded_ref[i].astype(F32)
        return carry

    lax.fori_loop(0, rows + 2 * MARGIN, unpack, 0)
    for tap in range(TAPS * TAPS):
        wts[tap] = jnp.broadcast_to(dw_ref[tap : tap + 1, :], (8, channels))

    def conv_body(block, carry):
        start = block * 8
        total = [jnp.broadcast_to(dw_bias, (8, channels)) for _ in range(rows)]
        for b in range(TAPS):
            xs = [xf[line, pl.ds(start + b, 8), :] for line in range(rows + TAPS - 1)]
            for a in range(TAPS):
                wv = wts[a * TAPS + b]
                for r in range(rows):
                    total[r] = total[r] + xs[r + a] * wv
        for r in range(rows):
            conv[r, pl.ds(pl.multiple_of(start, 8), 8), :] = total[r]
        return carry

    lax.fori_loop(0, cols // 8, conv_body, 0)

    land = land_ref[...].astype(F32)
    line_id = lax.broadcasted_iota(I32, land.shape, 0)
    ones = jnp.ones((rows, channels), BF16)

    def tile_body(r, carry):
        field = conv[r]
        centred = field - jnp.mean(field, axis=-1, keepdims=True)
        inv_std = lax.rsqrt(jnp.mean(centred * centred, axis=-1, keepdims=True) + 1e-06)
        normed = centred * inv_std
        norm[...] = normed
        mixed = (normed * gain + shift + forcing_ref[r].astype(F32)).astype(BF16)
        own_line = jnp.where(line_id == r, land, 0.0).astype(BF16)
        ocean = lax.dot_general(
            own_line, ones, (((0,), (0,)), ((), ())), preferred_element_type=F32
        )
        grad_out = (ocean * scale * cot_ref[r].astype(F32)).astype(BF16)
        pre[...] = nn_dot(mixed, up_ref[...]) + up_bias_ref[...]
        gh[...] = nt_dot(grad_out, down_ref[...])

        def gelu_body(i, carry):
            start = pl.multiple_of(i * 64, 64)
            p = pre[pl.ds(start, 64), :]
            u = p * p
            half = 0.5 + 0.5 * jnp.tanh(p * (gelu_scale + gelu_scale * cubic_coef * u))
            value = p * half
            slope = half + value * (1.0 - half) * (
                2.0 * gelu_scale + 6.0 * gelu_scale * cubic_coef * u
            )
            hid[pl.ds(start, 64), :] = value.astype(BF16)
            gp[pl.ds(start, 64), :] = (gh[pl.ds(start, 64), :] * slope).astype(BF16)
            return carry

        lax.fori_loop(0, cols // 64, gelu_body, 0)
        hidden = hid[...]
        grad_pre = gp[...]
        projected = nn_dot(hidden, down_ref[...]) + down_bias
        result_ref[r] = (ocean * (state_ref[r].astype(F32) + scale * projected)).astype(BF16)
        down_acc[...] += nn_dot(grad_out.T, hidden)
        up_acc[...] += nn_dot(mixed.T, grad_pre)
        grad_mixed = nt_dot(grad_pre, up_ref[...])
        gm[pl.ds(pl.multiple_of(r * cols, cols), cols), :] = grad_mixed
        gained = grad_mixed * gain
        normed2 = norm[...]
        back = (
            gained
            - jnp.mean(gained, axis=-1, keepdims=True)
            - normed2 * jnp.mean(gained * normed2, axis=-1, keepdims=True)
        ) * inv_std
        gconv_ref[r] = back.astype(BF16)
        return carry

    lax.fori_loop(0, rows, tile_body, 0)

    unit = 16

    def pack_body(i, carry):
        first = i * unit
        for k in range(unit):
            line = gm[pl.ds(first + k, 1), :]
            for j in range(2):
                entry = 2 * first + 2 * k + j
                buf[pl.ds(slot_ref[entry], 1), :] = line
        return carry

    lax.fori_loop(0, rows * cols // unit, pack_body, 0)

    for blk in range(hidden_units // LANES):
        parts_ref[blk] = up_acc[:, blk * LANES : (blk + 1) * LANES].astype(BF16)
        parts_ref[4 + blk] = down_acc[:, blk * LANES : (blk + 1) * LANES].T.astype(BF16)
    group = 8

    def cast_body(i, carry):
        for k in range(group):
            start = pl.multiple_of((i * group + k) * CAP, CAP)
            send_ref[i * group + k] = buf[pl.ds(start, CAP), :].astype(BF16)
        return carry

    lax.fori_loop(0, DEVICES // group, cast_body, 0)


def run_block(padded, state, forcing, cotangent, land, dw, chan, up, up_bias, down, slots):
    rows, cols, channels = state.shape
    hidden = up.shape[1]
    wide = padded.shape[1]
    lines = padded.shape[0]
    return pl.pallas_call(
        block_kernel,
        out_shape=(
            jax.ShapeDtypeStruct(state.shape, BF16),
            jax.ShapeDtypeStruct((LAT, LANES, LANES), BF16),
            jax.ShapeDtypeStruct((DEVICES, CAP, channels), BF16),
            jax.ShapeDtypeStruct(state.shape, BF16),
        ),
        in_specs=[VMEM_SPEC] * 10 + [SMEM_SPEC],
        out_specs=[VMEM_SPEC] * 4,
        scratch_shapes=[
            pltpu.VMEM((lines, wide, channels), F32),
            pltpu.VMEM((TAPS * TAPS, 8, channels), F32),
            pltpu.VMEM((rows, cols, channels), F32),
            pltpu.VMEM((rows * cols, channels), F32),
            pltpu.VMEM((cols, hidden), F32),
            pltpu.VMEM((cols, hidden), F32),
            pltpu.VMEM((cols, hidden), BF16),
            pltpu.VMEM((cols, hidden), BF16),
            pltpu.VMEM((cols, channels), F32),
            pltpu.VMEM((channels, hidden), F32),
            pltpu.VMEM((channels, hidden), F32),
            pltpu.VMEM((DEVICES * CAP, channels), F32),
        ],
        name="block_pass",
        cost_estimate=pl.CostEstimate(
            flops=3 * 10**9, bytes_accessed=10**7, transcendentals=rows * cols * hidden
        ),
    )(padded, state, forcing, cotangent, land, dw, chan, up, up_bias, down, slots)


def exchange_kernel(
    rows_hbm,
    cells_hbm,
    parts_ref,
    padded_ref,
    gconv_ref,
    table_ref,
    chunks_ref,
    grad_ref,
    xf,
    gf,
    recv_rows,
    recv_cells,
    recv1,
    dw_part,
    recv_dw,
    send2,
    recv2,
    send3,
    recv3,
    send4,
    recv4,
    row_send,
    row_recv,
    cell_send,
    cell_recv,
    send_sem,
    recv_sem,
    entered,
):
    lat = lax.axis_index("lat")
    lon = lax.axis_index("lon")
    me = lat * LON + lon

    def device(k):
        peer = lax.rem(me + k * STRIDE, DEVICES)
        return (peer // LON, lax.rem(peer, LON))

    barrier = pltpu.get_barrier_semaphore()

    def greet_lon(k, carry):
        to = (lat, lax.rem(lon + k, LON))
        pl.semaphore_signal(barrier, inc=1, device_id=to, device_id_type=MESH)
        return carry

    def greet_lat(k, carry):
        to = (lax.rem(lat + k, LAT), lon)
        pl.semaphore_signal(barrier, inc=1, device_id=to, device_id_type=MESH)
        return carry

    def pass_on(k, carry):
        to = (lax.rem(lat + k, LAT), lon)
        pl.semaphore_signal(entered, inc=1, device_id=to, device_id_type=MESH)
        return carry

    lax.fori_loop(1, LON, greet_lon, 0)
    lax.fori_loop(1, LAT, greet_lat, 0)

    recv_rows[:, CAP:, :] = jnp.zeros((DEVICES, LANES - CAP, LANES), BF16)
    grad_ref[...] = jnp.zeros_like(grad_ref)
    pl.semaphore_wait(barrier, LON + LAT - 2)
    lax.fori_loop(1, LAT, pass_on, 0)
    pl.semaphore_wait(entered, LAT - 1)

    def row_copy(k):
        to = device(k)
        peer = to[0] * LON + to[1]
        return (
            pltpu.make_async_remote_copy(
                src_ref=rows_hbm.at[peer],
                dst_ref=recv_rows.at[k, pl.ds(0, CAP)],
                send_sem=row_send.at[k],
                recv_sem=row_recv.at[k],
                device_id=to,
                device_id_type=MESH,
            ),
            pltpu.make_async_remote_copy(
                src_ref=cells_hbm.at[peer],
                dst_ref=recv_cells.at[k],
                send_sem=cell_send.at[k],
                recv_sem=cell_recv.at[k],
                device_id=to,
                device_id_type=MESH,
            ),
        )

    def send_range(first, last):
        def body(k, carry):
            for copy in row_copy(k):
                copy.start()
            return carry

        lax.fori_loop(first, last, body, 0)

    own_rows = pltpu.make_async_copy(rows_hbm.at[me], recv_rows.at[0, pl.ds(0, CAP)], row_recv.at[0])
    own_cells = pltpu.make_async_copy(cells_hbm.at[me], recv_cells.at[0], cell_recv.at[0])

    def lat_copy(stage, k, src, dst):
        to = lax.rem(lat + k, LAT)
        return pltpu.make_async_remote_copy(
            src_ref=src(to),
            dst_ref=dst.at[k],
            send_sem=send_sem.at[stage, k],
            recv_sem=recv_sem.at[stage, k],
            device_id=(to, lon),
            device_id_type=MESH,
        )

    def lon_copy(stage, k, src, dst):
        to = lax.rem(lon + k, LON)
        return pltpu.make_async_remote_copy(
            src_ref=src(to),
            dst_ref=dst.at[k],
            send_sem=send_sem.at[stage, k],
            recv_sem=recv_sem.at[stage, k],
            device_id=(lat, to),
            device_id_type=MESH,
        )

    def copy1(k):
        return lat_copy(0, k, lambda to: parts_ref.at[to], recv1)

    def copy_dw(k):
        return lat_copy(4, k, lambda to: dw_part.at[to], recv_dw)

    def copy2(k):
        return lon_copy(1, k, lambda to: send2.at[to], recv2)

    def copy3(k):
        return lon_copy(2, k, lambda to: send3, recv3)

    def copy4(k):
        return lat_copy(3, k, lambda to: send4, recv4)

    def start_all(copy, count):
        def body(k, carry):
            copy(k).start()
            return carry

        lax.fori_loop(1, count, body, 0)

    def arrive_all(copy, count):
        def body(k, carry):
            copy(k).wait_recv()
            return carry

        lax.fori_loop(1, count, body, 0)

    def left_all(copy, count):
        def body(k, carry):
            copy(k).wait_send()
            return carry

        lax.fori_loop(1, count, body, 0)

    start_all(copy1, LAT)
    own_rows.start()
    own_cells.start()
    send_range(1, 40)

    lines, wide, channels = xf.shape
    out_lines, cols = gf.shape[0], gf.shape[1]

    def unpack_x(i, carry):
        xf[i] = padded_ref[i].astype(F32)
        return carry

    def unpack_g(i, carry):
        gf[i] = gconv_ref[i].astype(F32)
        return carry

    lax.fori_loop(0, lines, unpack_x, 0)
    lax.fori_loop(0, out_lines, unpack_g, 0)
    sums = [[None] * TAPS for _ in range(TAPS)]
    for b in range(TAPS):

        def corr_body(block, carry):
            start = block * 8
            xs = [xf[line, pl.ds(start + b, 8), :] for line in range(lines)]
            gs = [gf[r, pl.ds(pl.multiple_of(start, 8), 8), :] for r in range(out_lines)]
            out = []
            for a in range(TAPS):
                total = carry[a]
                for r in range(out_lines):
                    total = total + xs[r + a] * gs[r]
                out.append(total)
            return tuple(out)

        done = lax.fori_loop(
            0, cols // 8, corr_body, tuple(jnp.zeros((8, channels), F32) for _ in range(TAPS))
        )
        for a in range(TAPS):
            sums[a][b] = jnp.sum(done[a], axis=0, keepdims=True)
    for a in range(TAPS):
        lines_a = sums[a] + [jnp.zeros((DW_ROWS - TAPS, channels), F32)]
        dw_part[a] = jnp.concatenate(lines_a, axis=0).astype(BF16)
    dw_part[TAPS] = jnp.zeros((DW_ROWS, channels), BF16)

    start_all(copy_dw, LAT)
    send_range(40, 64)
    arrive_all(copy1, LAT)
    arrive_all(copy_dw, LAT)
    total = parts_ref[lat].astype(F32)
    tail = dw_part[lat].astype(F32)
    for k in range(1, LAT):
        total = total + recv1[k].astype(F32)
        tail = tail + recv_dw[k].astype(F32)
    tail = tail[:8, :]
    for j in range(LON):
        send2[j] = jnp.concatenate([total[8 * j : 8 * j + 8, :], tail], axis=0).astype(BF16)

    start_all(copy2, LON)
    send_range(64, 88)
    arrive_all(copy2, LON)
    total = send2[lon].astype(F32)
    for k in range(1, LON):
        total = total + recv2[k].astype(F32)
    send3[...] = total[:8, :]
    send4[LANES:, :] = jnp.concatenate([total[8:, :], jnp.zeros((8, LANES), F32)], axis=0).astype(BF16)

    start_all(copy3, LON)
    send_range(88, DEVICES)
    arrive_all(copy3, LON)
    recv3[0] = send3[...]
    for j in range(LON // 2):
        pair = [recv3[lax.rem(lon - (2 * j + i) + LON, LON)] for i in range(2)]
        send4[16 * j : 16 * j + 16, :] = jnp.concatenate(pair, axis=0).astype(BF16)

    start_all(copy4, LAT)

    cell_id = lax.broadcasted_iota(I32, (A_DEV, LANES), 0)

    def add_pair(i):
        parts = []
        for j in range(2):
            code = recv_cells[2 * i + j]
            index = code >> CODE_BITS
            weight = jnp.zeros(code.shape, F32)
            for entry in range(table_ref.shape[0]):
                weight = jnp.where(index == entry, table_ref[entry], weight)
            cell = jnp.where(code < 0, -1, code & (A_DEV - 1))
            parts.append(jnp.where(cell_id == cell, weight, 0.0).astype(BF16))
        hot = jnp.concatenate(parts, axis=1)
        values = recv_rows[pl.ds(2 * i, 2)].reshape(2 * LANES, LANES)
        grad_ref[...] += nn_dot(hot, values)

    def wait_rows(k):
        for copy in row_copy(k):
            copy.wait_recv()

    own_rows.wait()
    own_cells.wait()
    wait_rows(1)
    add_pair(0)

    def pair_body(i, carry):
        wait_rows(2 * i)
        wait_rows(2 * i + 1)
        add_pair(i)
        return carry

    lax.fori_loop(1, DEVICES // 2, pair_body, 0)

    arrive_all(copy4, LAT)
    recv4[0] = send4[...]
    for chunk in range(LAT):
        chunks_ref[chunk] = recv4[lax.rem(lat - chunk + LAT, LAT)]

    left_all(copy1, LAT)
    left_all(copy_dw, LAT)
    left_all(copy2, LON)
    left_all(copy3, LON)
    left_all(copy4, LAT)

    def left_body(k, carry):
        for copy in row_copy(k):
            copy.wait_send()
        return carry

    lax.fori_loop(1, DEVICES, left_body, 0)


def exchange(rows, cells, parts, padded, gconv, table):
    dma = pltpu.SemaphoreType.DMA
    return pl.pallas_call(
        exchange_kernel,
        out_shape=(
            jax.ShapeDtypeStruct((LAT, PART_ROWS, LANES), BF16),
            jax.ShapeDtypeStruct((A_DEV, LANES), F32),
        ),
        in_specs=[ANY_SPEC, ANY_SPEC, VMEM_SPEC, VMEM_SPEC, VMEM_SPEC, SMEM_SPEC],
        out_specs=[VMEM_SPEC] * 2,
        scratch_shapes=[
            pltpu.VMEM(padded.shape, F32),
            pltpu.VMEM(gconv.shape, F32),
            pltpu.VMEM((DEVICES, LANES, LANES), BF16),
            pltpu.VMEM((DEVICES, 1, LANES), I32),
            pltpu.VMEM((LAT, LANES, LANES), BF16),
            pltpu.VMEM((LAT, DW_ROWS, LANES), BF16),
            pltpu.VMEM((LAT, DW_ROWS, LANES), BF16),
            pltpu.VMEM((LON, 16, LANES), BF16),
            pltpu.VMEM((LON, 16, LANES), BF16),
            pltpu.VMEM((8, LANES), F32),
            pltpu.VMEM((LON, 8, LANES), F32),
            pltpu.VMEM((PART_ROWS, LANES), BF16),
            pltpu.VMEM((LAT, PART_ROWS, LANES), BF16),
            dma((DEVICES,)),
            dma((DEVICES,)),
            dma((DEVICES,)),
            dma((DEVICES,)),
            dma((5, LON)),
            dma((5, LON)),
            pltpu.SemaphoreType.REGULAR,
        ],
        compiler_params=pltpu.CompilerParams(collective_id=0, has_side_effects=True),
        name="exchange",
    )(rows, cells.reshape(DEVICES, 1, LANES), parts, padded, gconv, table)


def finish_kernel(factor, chunks_ref, grad_ref, up_ref, down_ref, dw_ref, out_ref):
    for chunk in range(LAT):
        block = chunks_ref[chunk].astype(F32) * factor
        if chunk < 4:
            up_ref[:, chunk * LANES : (chunk + 1) * LANES] = block[:LANES]
        else:
            down_ref[(chunk - 4) * LANES : (chunk - 3) * LANES, :] = block[:LANES]
        if chunk < TAPS:
            dw_ref[chunk] = block[LANES : LANES + TAPS]
    out_ref[...] = grad_ref[...]


def finish(chunks, grad, factor):
    return pl.pallas_call(
        functools.partial(finish_kernel, factor),
        out_shape=(
            jax.ShapeDtypeStruct((LANES, 512), F32),
            jax.ShapeDtypeStruct((512, LANES), F32),
            jax.ShapeDtypeStruct((TAPS, TAPS, LANES), F32),
            jax.ShapeDtypeStruct((A_DEV, LANES), F32),
        ),
        in_specs=[VMEM_SPEC] * 2,
        out_specs=[VMEM_SPEC] * 4,
        name="finish",
    )(chunks, grad)


def extended(block, sides, width, periodic):
    for axis, dim in sides:
        count = lax.axis_size(axis)
        forward = [(i, i + 1) for i in range(count - 1)]
        if periodic:
            forward.append((count - 1, 0))
        backward = [(target, source) for source, target in forward]
        low = lax.ppermute(
            lax.slice_in_dim(block, block.shape[dim] - width, None, axis=dim), axis, forward
        )
        high = lax.ppermute(lax.slice_in_dim(block, 0, width, axis=dim), axis, backward)
        block = jnp.concatenate([low, block, high], axis=dim)
    return block


def on_device(
    state,
    forcing,
    cotangent,
    land_mask,
    dw_weight,
    dw_bias,
    norm_gain,
    norm_bias,
    up_weight,
    up_bias,
    down_weight,
    down_bias,
    layer_scale,
    owner,
    atmos_cell,
    weight_index,
    intersection_weights,
):
    rows, cols, channels = state.shape
    slots, cells = rank_entries(owner[:, 0], atmos_cell, weight_index)

    lon_ext = extended(state, (("lon", 1),), MARGIN, True)
    padded = extended(lon_ext, (("lat", 0),), MARGIN, False)
    partner = lax.ppermute(
        lon_ext[rows - MARGIN :], "lon", [(i, LON - 1 - i) for i in range(LON)]
    )
    mirrored = partner[::-1, ::-1]
    northmost = lax.axis_index("lat") == LAT - 1
    north_rows = jnp.where(northmost, mirrored, padded[rows + MARGIN :])
    padded = jnp.concatenate([padded[: rows + MARGIN], north_rows], axis=0)
    padded = jnp.pad(padded, ((0, 0), (0, 2), (0, 0)))

    chan = jnp.stack(
        [dw_bias, norm_gain, norm_bias, down_bias, layer_scale] + [jnp.zeros_like(dw_bias)] * 3
    )
    result, parts, send_rows, gconv = run_block(
        padded,
        state,
        forcing,
        cotangent,
        land_mask,
        dw_weight.astype(F32).reshape(TAPS * TAPS, channels),
        chan,
        up_weight,
        up_bias.reshape(1, -1),
        down_weight,
        slots.reshape(-1),
    )
    factor = float(rows * LAT * cols * LON) ** (-0.5)
    chunks, grad = exchange(send_rows, cells, parts, padded, gconv, intersection_weights)
    grad_up, grad_down, grad_dw, forcing_grad = finish(chunks, grad, factor)
    return (result, grad_dw, grad_up, grad_down, forcing_grad)


def solution(mesh):
    in_specs = (
        P("lat", "lon", None),
        P("lat", "lon", None),
        P("lat", "lon", None),
        P("lat", "lon"),
        P(),
        P(),
        P(),
        P(),
        P(),
        P(),
        P(),
        P(),
        P(),
        P(("lat", "lon"), None),
        P(("lat", "lon")),
        P(("lat", "lon")),
        P(),
    )
    out_specs = (P("lat", "lon", None), P(), P(), P(), P(("lat", "lon"), None))
    return jax.shard_map(
        on_device, mesh=mesh, in_specs=in_specs, out_specs=out_specs, check_vma=False
    )
```

```python
import functools

import jax
import jax.numpy as jnp
from jax import lax
from jax.experimental import pallas as pl
from jax.experimental.pallas import tpu as pltpu
from jax.sharding import PartitionSpec as P

F32 = jnp.float32
BF16 = jnp.bfloat16
I32 = jnp.int32
MESH = pl.DeviceIdType.MESH
VMEM_SPEC = pl.BlockSpec(memory_space=pltpu.VMEM)
SMEM_SPEC = pl.BlockSpec(memory_space=pltpu.SMEM)
ANY_SPEC = pl.BlockSpec(memory_space=pl.ANY)

A_DEV = 512
LANES = 128
CAP = 96
MARGIN = 3
TAPS = 7
LAT = 8
LON = 16
DEVICES = LAT * LON
PART_ROWS = 144
STRIDE = 77
EDGE = 16
GROUP = 8
DW_ROWS = 16
CODE_BITS = 9

gelu_scale = 0.7978845608028654
cubic_coef = 0.044715


def nt_dot(a, b):
    return lax.dot_general(a, b, (((1,), (1,)), ((), ())), preferred_element_type=F32)


def nn_dot(a, b):
    return jnp.dot(a, b, preferred_element_type=F32)


def rank_body(owner_ref, cell_ref, index_ref, slot_ref, cells_ref, base, acc):
    blocks = owner_ref.shape[0]
    group = 8
    base[...] = jnp.zeros_like(base)
    acc[...] = jnp.zeros_like(acc)
    row_id = lax.broadcasted_iota(I32, (LANES, LANES), 0)
    col_id = lax.broadcasted_iota(I32, (LANES, LANES), 1)
    tri = jnp.concatenate(
        [jnp.where(row_id < col_id, 1.0, 0.0), jnp.ones((LANES, LANES), F32)], axis=1
    ).astype(BF16)

    def body(step, carry):
        start = pl.multiple_of(step * group, group)
        owners = owner_ref[pl.ds(start, group), :]
        coded = cell_ref[pl.ds(start, group), :] + (index_ref[pl.ds(start, group), :] << CODE_BITS) + 1
        high = (coded >> 7).astype(F32)
        low = (coded & 127).astype(F32)
        ranks = []
        for i in range(group):
            hit = row_id == owners[i : i + 1, :]
            hot = jnp.where(hit, 1.0, 0.0)
            hot16 = hot.astype(BF16)
            sums = nn_dot(hot16, tri)
            before = sums[:, :LANES] + base[...]
            rank = jnp.sum(hot * before, axis=0, keepdims=True)
            ranks.append(rank)
            base[...] += sums[:, LANES:]
            at_rank = row_id == rank.astype(I32)
            spread = jnp.concatenate(
                [
                    jnp.where(at_rank, high[i : i + 1, :], 0.0),
                    jnp.where(at_rank, low[i : i + 1, :], 0.0),
                ],
                axis=0,
            ).astype(BF16)
            acc[...] += nt_dot(hot16, spread)
        rank8 = jnp.concatenate(ranks, axis=0).astype(I32)
        slot_ref[pl.ds(start, group), :] = owners * CAP + rank8
        return carry

    lax.fori_loop(0, blocks // group, body, 0)
    total = acc[...]
    cells_ref[...] = (128.0 * total[:, :LANES] + total[:, LANES:]).astype(I32) - 1


def halo_kernel(
    state_ref,
    owner_ref,
    cell_ref,
    index_ref,
    pad_ref,
    slot_ref,
    cells_ref,
    base,
    acc,
    from_left,
    from_right,
    from_up,
    from_down,
    up_left,
    up_right,
    down_left,
    down_right,
    send_sem,
    recv_sem,
):
    lat = lax.axis_index("lat")
    lon = lax.axis_index("lon")
    rows, cols, channels = state_ref.shape
    left = (lat, lax.rem(lon + LON - 1, LON))
    right = (lat, lax.rem(lon + 1, LON))
    above = (lat + 1, lon)
    below = (lat - 1, lon)
    fold = (lat, LON - 1 - lon)
    top = rows - MARGIN
    inner = lat < LAT - 1
    folded = lat == LAT - 1
    lower = lat > 0

    barrier = pltpu.get_barrier_semaphore()

    def greet(to):
        pl.semaphore_signal(barrier, inc=1, device_id=to, device_id_type=MESH)

    greet(left)
    greet(right)

    @pl.when(inner)
    def _():
        greet(above)

    @pl.when(folded)
    def _():
        greet(fold)

    @pl.when(lower)
    def _():
        greet(below)
        pl.semaphore_wait(barrier, 4)

    @pl.when(lat == 0)
    def _():
        pl.semaphore_wait(barrier, 3)

    def copy(number, src, dst, to):
        return pltpu.make_async_remote_copy(
            src_ref=src,
            dst_ref=dst[0],
            send_sem=send_sem.at[number],
            recv_sem=recv_sem.at[dst[1]],
            device_id=to,
            device_id_type=MESH,
        )

    bottom_rows = state_ref.at[pl.ds(0, MARGIN)]
    top_rows = state_ref.at[pl.ds(top, MARGIN)]
    to_left = copy(0, state_ref.at[:, pl.ds(0, EDGE)], (from_right, 0), left)
    to_right = copy(1, state_ref.at[:, pl.ds(cols - EDGE, EDGE)], (from_left, 1), right)
    down_main = copy(2, bottom_rows, (from_up, 2), below)
    up_main = copy(3, top_rows, (from_down, 3), above)
    fold_main = copy(3, top_rows, (from_up, 2), fold)
    down_l = copy(4, from_left.at[pl.ds(0, MARGIN)], (up_left, 4), below)
    down_r = copy(5, from_right.at[pl.ds(0, MARGIN)], (up_right, 5), below)
    up_l = copy(6, from_left.at[pl.ds(top, MARGIN)], (down_left, 6), above)
    up_r = copy(7, from_right.at[pl.ds(top, MARGIN)], (down_right, 7), above)
    fold_l = copy(6, from_left.at[pl.ds(top, MARGIN)], (up_right, 5), fold)
    fold_r = copy(7, from_right.at[pl.ds(top, MARGIN)], (up_left, 4), fold)

    to_left.start()
    to_right.start()

    @pl.when(lower)
    def _():
        down_main.start()

    @pl.when(inner)
    def _():
        up_main.start()

    @pl.when(folded)
    def _():
        fold_main.start()

    to_left.wait_recv()
    to_right.wait_recv()

    @pl.when(lower)
    def _():
        down_l.start()
        down_r.start()

    @pl.when(inner)
    def _():
        up_l.start()
        up_r.start()

    @pl.when(folded)
    def _():
        fold_l.start()
        fold_r.start()

    right_at = MARGIN + cols

    def place(line, main, on_left, on_right):
        pad_ref[line, MARGIN:right_at, :] = main.astype(F32)
        pad_ref[line, 0:MARGIN, :] = on_left.astype(F32)[EDGE - MARGIN :]
        pad_ref[line, right_at : right_at + MARGIN, :] = on_right.astype(F32)[:MARGIN]

    pad_ref[:, right_at + MARGIN :, :] = jnp.zeros(
        (rows + 2 * MARGIN, pad_ref.shape[1] - right_at - MARGIN, channels), F32
    )
    for r in range(rows):
        place(MARGIN + r, state_ref[r], from_left[r], from_right[r])

    rank_body(owner_ref, cell_ref, index_ref, slot_ref, cells_ref, base, acc)

    down_main.wait_recv()
    down_l.wait_recv()
    down_r.wait_recv()

    @pl.when(inner)
    def _():
        for m in range(MARGIN):
            place(MARGIN + rows + m, from_up[m], up_left[m], up_right[m])

    @pl.when(folded)
    def _():
        def flip(size):
            ids = [lax.broadcasted_iota(I32, (size, size), d) for d in range(2)]
            return jnp.where(ids[0] + ids[1] == size - 1, 1.0, 0.0).astype(BF16)

        swap = flip(LANES)
        swap_edge = flip(EDGE)
        for m in range(MARGIN):
            line = MARGIN + rows + m
            source = MARGIN - 1 - m
            for q in range(cols // LANES):
                first = cols - (q + 1) * LANES
                pad_ref[line, MARGIN + q * LANES : MARGIN + (q + 1) * LANES, :] = nn_dot(
                    swap, from_up[source, first : first + LANES, :]
                )
            pad_ref[line, 0:MARGIN, :] = nn_dot(swap_edge, up_left[source])[EDGE - MARGIN :]
            pad_ref[line, right_at : right_at + MARGIN, :] = nn_dot(swap_edge, up_right[source])[:MARGIN]

    @pl.when(lower)
    def _():
        up_main.wait_recv()
        up_l.wait_recv()
        up_r.wait_recv()
        for m in range(MARGIN):
            place(m, from_down[m], down_left[m], down_right[m])

    @pl.when(lat == 0)
    def _():
        pad_ref[0:MARGIN] = jnp.zeros((MARGIN,) + pad_ref.shape[1:], F32)

    to_left.wait_send()
    to_right.wait_send()
    up_main.wait_send()
    up_l.wait_send()
    up_r.wait_send()

    @pl.when(lower)
    def _():
        down_main.wait_send()
        down_l.wait_send()
        down_r.wait_send()


def exchange_halo(state, owner, atmos_cell, weight_index):
    rows, cols, channels = state.shape
    entries = owner.shape[0]
    shape = (entries // LANES, LANES)
    dma = pltpu.SemaphoreType.DMA
    edge = pltpu.VMEM((rows, EDGE, channels), BF16)
    strip = pltpu.VMEM((MARGIN, cols, channels), BF16)
    corner = pltpu.VMEM((MARGIN, EDGE, channels), BF16)
    return pl.pallas_call(
        halo_kernel,
        out_shape=(
            jax.ShapeDtypeStruct((rows + 2 * MARGIN, cols + 8, channels), F32),
            jax.ShapeDtypeStruct(shape, I32),
            jax.ShapeDtypeStruct((DEVICES, LANES), I32),
        ),
        in_specs=[VMEM_SPEC] * 4,
        out_specs=[VMEM_SPEC] * 3,
        scratch_shapes=[
            pltpu.VMEM((LANES, LANES), F32),
            pltpu.VMEM((LANES, 2 * LANES), F32),
            edge,
            edge,
            strip,
            strip,
            corner,
            corner,
            corner,
            corner,
            dma((8,)),
            dma((8,)),
        ],
        compiler_params=pltpu.CompilerParams(collective_id=1, has_side_effects=True),
        name="exchange_halo",
    )(state, owner.reshape(shape), atmos_cell.reshape(shape), weight_index.reshape(shape))


def block_kernel(
    padded_ref,
    state_ref,
    forcing_ref,
    cot_ref,
    land_ref,
    dw_ref,
    dw_bias_ref,
    gain_ref,
    shift_ref,
    down_bias_ref,
    scale_ref,
    up_ref,
    up_bias_ref,
    down_ref,
    slot_ref,
    result_ref,
    parts_ref,
    send_ref,
    gconv_ref,
    wts,
    conv,
    gm,
    pre,
    gh,
    hid,
    gp,
    norm,
    up_acc,
    down_acc,
    buf,
):
    rows, cols, channels = state_ref.shape
    hidden_units = up_ref.shape[1]
    dw_bias = dw_bias_ref[...]
    gain = gain_ref[...]
    shift = shift_ref[...]
    down_bias = down_bias_ref[...]
    scale = scale_ref[...]

    def zero_body(i, carry):
        buf[pl.ds(pl.multiple_of(i * 128, 128), 128), :] = jnp.zeros((128, channels), F32)
        return carry

    lax.fori_loop(0, buf.shape[0] // 128, zero_body, 0)
    up_acc[...] = jnp.zeros_like(up_acc)
    down_acc[...] = jnp.zeros_like(down_acc)

    for a in range(TAPS):
        taps = dw_ref[a].astype(F32)
        for b in range(TAPS):
            wts[a * TAPS + b] = jnp.broadcast_to(taps[b : b + 1, :], (8, channels))

    def conv_body(block, carry):
        start = block * 8
        total = [jnp.broadcast_to(dw_bias, (8, channels)) for _ in range(rows)]
        for b in range(TAPS):
            xs = [padded_ref[line, pl.ds(start + b, 8), :] for line in range(rows + TAPS - 1)]
            for a in range(TAPS):
                wv = wts[a * TAPS + b]
                for r in range(rows):
                    total[r] = total[r] + xs[r + a] * wv
        for r in range(rows):
            conv[r, pl.ds(pl.multiple_of(start, 8), 8), :] = total[r]
        return carry

    lax.fori_loop(0, cols // 8, conv_body, 0)

    land = land_ref[...].astype(F32)
    line_id = lax.broadcasted_iota(I32, land.shape, 0)
    ones = jnp.ones((rows, channels), BF16)

    def tile_body(r, carry):
        field = conv[r]
        centred = field - jnp.mean(field, axis=-1, keepdims=True)
        inv_std = lax.rsqrt(jnp.mean(centred * centred, axis=-1, keepdims=True) + 1e-06)
        normed = centred * inv_std
        norm[...] = normed
        mixed = (normed * gain + shift + forcing_ref[r].astype(F32)).astype(BF16)
        own_line = jnp.where(line_id == r, land, 0.0).astype(BF16)
        ocean = lax.dot_general(
            own_line, ones, (((0,), (0,)), ((), ())), preferred_element_type=F32
        )
        grad_out = (ocean * scale * cot_ref[r].astype(F32)).astype(BF16)
        pre[...] = nn_dot(mixed, up_ref[...]) + up_bias_ref[...]
        gh[...] = nt_dot(grad_out, down_ref[...])

        def gelu_body(i, carry):
            start = pl.multiple_of(i * 64, 64)
            p = pre[pl.ds(start, 64), :]
            u = p * p
            half = 0.5 + 0.5 * jnp.tanh(p * (gelu_scale + gelu_scale * cubic_coef * u))
            value = p * half
            slope = half + value * (1.0 - half) * (
                2.0 * gelu_scale + 6.0 * gelu_scale * cubic_coef * u
            )
            hid[pl.ds(start, 64), :] = value.astype(BF16)
            gp[pl.ds(start, 64), :] = (gh[pl.ds(start, 64), :] * slope).astype(BF16)
            return carry

        lax.fori_loop(0, cols // 64, gelu_body, 0)
        hidden = hid[...]
        grad_pre = gp[...]
        projected = nn_dot(hidden, down_ref[...]) + down_bias
        result_ref[r] = (ocean * (state_ref[r].astype(F32) + scale * projected)).astype(BF16)
        down_acc[...] += nn_dot(grad_out.T, hidden)
        up_acc[...] += nn_dot(mixed.T, grad_pre)
        grad_mixed = nt_dot(grad_pre, up_ref[...])
        gm[pl.ds(pl.multiple_of(r * cols, cols), cols), :] = grad_mixed
        gained = grad_mixed * gain
        normed2 = norm[...]
        back = (
            gained
            - jnp.mean(gained, axis=-1, keepdims=True)
            - normed2 * jnp.mean(gained * normed2, axis=-1, keepdims=True)
        ) * inv_std
        gconv_ref[r] = back.astype(BF16)
        return carry

    lax.fori_loop(0, rows, tile_body, 0)

    unit = 16

    def pack_body(i, carry):
        first = i * unit
        for k in range(unit):
            line = gm[pl.ds(first + k, 1), :]
            for j in range(2):
                entry = 2 * first + 2 * k + j
                buf[pl.ds(slot_ref[entry], 1), :] = line
        return carry

    lax.fori_loop(0, rows * cols // unit, pack_body, 0)

    for blk in range(hidden_units // LANES):
        parts_ref[blk] = up_acc[:, blk * LANES : (blk + 1) * LANES].astype(BF16)
        parts_ref[4 + blk] = down_acc[:, blk * LANES : (blk + 1) * LANES].T.astype(BF16)
    group = 8

    def cast_body(i, carry):
        for k in range(group):
            start = pl.multiple_of((i * group + k) * CAP, CAP)
            send_ref[i * group + k] = buf[pl.ds(start, CAP), :].astype(BF16)
        return carry

    lax.fori_loop(0, DEVICES // group, cast_body, 0)


def run_block(padded, state, forcing, cotangent, land, dw, vectors, up, up_bias, down, slots):
    rows, cols, channels = state.shape
    hidden = up.shape[1]
    return pl.pallas_call(
        block_kernel,
        out_shape=(
            jax.ShapeDtypeStruct(state.shape, BF16),
            jax.ShapeDtypeStruct((LAT, LANES, LANES), BF16),
            jax.ShapeDtypeStruct((DEVICES, CAP, channels), BF16),
            jax.ShapeDtypeStruct(state.shape, BF16),
        ),
        in_specs=[VMEM_SPEC] * 14 + [SMEM_SPEC],
        out_specs=[VMEM_SPEC] * 4,
        scratch_shapes=[
            pltpu.VMEM((TAPS * TAPS, 8, channels), F32),
            pltpu.VMEM((rows, cols, channels), F32),
            pltpu.VMEM((rows * cols, channels), F32),
            pltpu.VMEM((cols, hidden), F32),
            pltpu.VMEM((cols, hidden), F32),
            pltpu.VMEM((cols, hidden), BF16),
            pltpu.VMEM((cols, hidden), BF16),
            pltpu.VMEM((cols, channels), F32),
            pltpu.VMEM((channels, hidden), F32),
            pltpu.VMEM((channels, hidden), F32),
            pltpu.VMEM((DEVICES * CAP, channels), F32),
        ],
        name="block_pass",
        cost_estimate=pl.CostEstimate(
            flops=3 * 10**9, bytes_accessed=10**7, transcendentals=rows * cols * hidden
        ),
    )(padded, state, forcing, cotangent, land, dw, *vectors, up, up_bias, down, slots)


def exchange_kernel(
    rows_hbm,
    cells_hbm,
    parts_ref,
    padded_ref,
    gconv_ref,
    table_ref,
    chunks_ref,
    grad_ref,
    gf,
    recv_rows,
    recv_cells,
    recv1,
    dw_part,
    recv_dw,
    send2,
    recv2,
    send3,
    recv3,
    send4,
    recv4,
    row_send,
    row_recv,
    cell_send,
    cell_recv,
    own_sem,
    send_sem,
    recv_sem,
    entered,
):
    lat = lax.axis_index("lat")
    lon = lax.axis_index("lon")
    me = lat * LON + lon

    def device(k):
        peer = lax.rem(me + k * STRIDE, DEVICES)
        return (peer // LON, lax.rem(peer, LON))

    barrier = pltpu.get_barrier_semaphore()

    def greet_lon(k, carry):
        to = (lat, lax.rem(lon + k, LON))
        pl.semaphore_signal(barrier, inc=1, device_id=to, device_id_type=MESH)
        return carry

    def greet_lat(k, carry):
        to = (lax.rem(lat + k, LAT), lon)
        pl.semaphore_signal(barrier, inc=1, device_id=to, device_id_type=MESH)
        return carry

    def pass_on(k, carry):
        to = (lax.rem(lat + k, LAT), lon)
        pl.semaphore_signal(entered, inc=1, device_id=to, device_id_type=MESH)
        return carry

    lax.fori_loop(1, LON, greet_lon, 0)
    lax.fori_loop(1, LAT, greet_lat, 0)

    def row_copy(k):
        to = device(k)
        return pltpu.make_async_remote_copy(
            src_ref=rows_hbm.at[to[0] * LON + to[1]],
            dst_ref=recv_rows.at[k, pl.ds(0, CAP)],
            send_sem=row_send.at[0],
            recv_sem=row_recv.at[k // GROUP],
            device_id=to,
            device_id_type=MESH,
        )

    def cell_copy(k):
        to = device(k)
        return pltpu.make_async_remote_copy(
            src_ref=cells_hbm.at[to[0] * LON + to[1]],
            dst_ref=recv_cells.at[k],
            send_sem=cell_send.at[0],
            recv_sem=cell_recv.at[0],
            device_id=to,
            device_id_type=MESH,
        )

    def send_range(first, last):
        def body(k, carry):
            row_copy(k).start()
            return carry

        lax.fori_loop(first, last, body, 0)

    def send_cells():
        def body(k, carry):
            cell_copy(k).start()
            return carry

        lax.fori_loop(1, DEVICES, body, 0)

    def await_bytes(ref, sem):
        pltpu.make_async_copy(ref, ref, sem).wait()

    own_rows = pltpu.make_async_copy(rows_hbm.at[me], recv_rows.at[0, pl.ds(0, CAP)], own_sem.at[0])
    own_cells = pltpu.make_async_copy(cells_hbm.at[me], recv_cells.at[0], own_sem.at[1])

    def lat_copy(stage, k, src, dst):
        to = lax.rem(lat + k, LAT)
        return pltpu.make_async_remote_copy(
            src_ref=src(to),
            dst_ref=dst.at[k],
            send_sem=send_sem.at[stage],
            recv_sem=recv_sem.at[stage],
            device_id=(to, lon),
            device_id_type=MESH,
        )

    def lon_copy(stage, k, src, dst):
        to = lax.rem(lon + k, LON)
        return pltpu.make_async_remote_copy(
            src_ref=src(to),
            dst_ref=dst.at[k],
            send_sem=send_sem.at[stage],
            recv_sem=recv_sem.at[stage],
            device_id=(lat, to),
            device_id_type=MESH,
        )

    def copy1(k):
        return lat_copy(0, k, lambda to: parts_ref.at[to], recv1)

    def copy_dw(k):
        return lat_copy(4, k, lambda to: dw_part.at[to], recv_dw)

    def copy2(k):
        return lon_copy(1, k, lambda to: send2.at[to], recv2)

    def copy3(k):
        return lon_copy(2, k, lambda to: send3, recv3)

    def copy4(k):
        return lat_copy(3, k, lambda to: send4, recv4)

    def start_all(copy, count):
        def body(k, carry):
            copy(k).start()
            return carry

        lax.fori_loop(1, count, body, 0)

    def arrive_all(stage, dst):
        await_bytes(dst.at[pl.ds(1, dst.shape[0] - 1)], recv_sem.at[stage])

    def left_all(stage, dst):
        await_bytes(dst.at[pl.ds(1, dst.shape[0] - 1)], send_sem.at[stage])

    own_rows.start()
    own_cells.start()
    recv_rows[:, CAP:, :] = jnp.zeros((DEVICES, LANES - CAP, LANES), BF16)
    grad_ref[...] = jnp.zeros_like(grad_ref)

    lines, wide, channels = padded_ref.shape
    out_lines, cols = gf.shape[0], gf.shape[1]

    def unpack_g(i, carry):
        gf[i] = gconv_ref[i].astype(F32)
        return carry

    lax.fori_loop(0, out_lines, unpack_g, 0)
    sums = [[None] * TAPS for _ in range(TAPS)]
    for b in range(TAPS):
        if b == 4:
            pl.semaphore_wait(barrier, LON + LAT - 2)
            lax.fori_loop(1, LAT, pass_on, 0)

        def corr_body(block, carry):
            start = block * 8
            xs = [padded_ref[line, pl.ds(start + b, 8), :] for line in range(lines)]
            gs = [gf[r, pl.ds(pl.multiple_of(start, 8), 8), :] for r in range(out_lines)]
            out = []
            for a in range(TAPS):
                total = carry[a]
                for r in range(out_lines):
                    total = total + xs[r + a] * gs[r]
                out.append(total)
            return tuple(out)

        done = lax.fori_loop(
            0, cols // 8, corr_body, tuple(jnp.zeros((8, channels), F32) for _ in range(TAPS))
        )
        for a in range(TAPS):
            sums[a][b] = jnp.sum(done[a], axis=0, keepdims=True)
    for a in range(TAPS):
        lines_a = sums[a] + [jnp.zeros((DW_ROWS - TAPS, channels), F32)]
        dw_part[a] = jnp.concatenate(lines_a, axis=0).astype(BF16)
    dw_part[TAPS] = jnp.zeros((DW_ROWS, channels), BF16)

    pl.semaphore_wait(entered, LAT - 1)

    start_all(copy1, LAT)
    start_all(copy_dw, LAT)
    send_cells()
    send_range(1, 24)
    arrive_all(0, recv1)
    arrive_all(4, recv_dw)
    total = parts_ref[lat].astype(F32)
    tail = dw_part[lat].astype(F32)
    for k in range(1, LAT):
        total = total + recv1[k].astype(F32)
        tail = tail + recv_dw[k].astype(F32)
    tail = tail[:8, :]
    for j in range(LON):
        send2[j] = jnp.concatenate([total[8 * j : 8 * j + 8, :], tail], axis=0).astype(BF16)

    start_all(copy2, LON)
    send_range(24, 48)
    arrive_all(1, recv2)
    total = send2[lon].astype(F32)
    for k in range(1, LON):
        total = total + recv2[k].astype(F32)
    send3[...] = total[:8, :]
    send4[LANES:, :] = jnp.concatenate([total[8:, :], jnp.zeros((8, LANES), F32)], axis=0).astype(BF16)

    start_all(copy3, LON)
    send_range(48, 72)
    arrive_all(2, recv3)
    recv3[0] = send3[...]
    for j in range(LON // 2):
        pair = [recv3[lax.rem(lon - (2 * j + i) + LON, LON)] for i in range(2)]
        send4[16 * j : 16 * j + 16, :] = jnp.concatenate(pair, axis=0).astype(BF16)

    start_all(copy4, LAT)
    send_range(72, DEVICES)

    cell_id = lax.broadcasted_iota(I32, (A_DEV, LANES), 0)

    def add_pair(i):
        parts = []
        for j in range(2):
            code = recv_cells[2 * i + j]
            index = code >> CODE_BITS
            weight = jnp.zeros(code.shape, F32)
            for entry in range(table_ref.shape[0]):
                weight = jnp.where(index == entry, table_ref[entry], weight)
            cell = jnp.where(code < 0, -1, code & (A_DEV - 1))
            parts.append(jnp.where(cell_id == cell, weight, 0.0).astype(BF16))
        hot = jnp.concatenate(parts, axis=1)
        values = recv_rows[pl.ds(2 * i, 2)].reshape(2 * LANES, LANES)
        grad_ref[...] += nn_dot(hot, values)

    own_rows.wait()
    own_cells.wait()
    await_bytes(recv_cells.at[pl.ds(1, DEVICES - 1)], cell_recv.at[0])
    await_bytes(recv_rows.at[pl.ds(1, GROUP - 1), pl.ds(0, CAP)], row_recv.at[0])
    for i in range(GROUP // 2):
        add_pair(i)

    def group_body(g, carry):
        await_bytes(recv_rows.at[pl.ds(g * GROUP, GROUP), pl.ds(0, CAP)], row_recv.at[g])
        for i in range(GROUP // 2):
            add_pair(g * (GROUP // 2) + i)
        return carry

    lax.fori_loop(1, DEVICES // GROUP, group_body, 0)

    arrive_all(3, recv4)
    recv4[0] = send4[...]
    for chunk in range(LAT):
        chunks_ref[chunk] = recv4[lax.rem(lat - chunk + LAT, LAT)]

    left_all(0, recv1)
    left_all(4, recv_dw)
    left_all(1, recv2)
    left_all(2, recv3)
    left_all(3, recv4)

    await_bytes(recv_rows.at[pl.ds(1, DEVICES - 1), pl.ds(0, CAP)], row_send.at[0])
    await_bytes(recv_cells.at[pl.ds(1, DEVICES - 1)], cell_send.at[0])


def exchange(rows, cells, parts, padded, gconv, table):
    dma = pltpu.SemaphoreType.DMA
    return pl.pallas_call(
        exchange_kernel,
        out_shape=(
            jax.ShapeDtypeStruct((LAT, PART_ROWS, LANES), BF16),
            jax.ShapeDtypeStruct((A_DEV, LANES), F32),
        ),
        in_specs=[ANY_SPEC, ANY_SPEC, VMEM_SPEC, VMEM_SPEC, VMEM_SPEC, SMEM_SPEC],
        out_specs=[VMEM_SPEC] * 2,
        scratch_shapes=[
            pltpu.VMEM(gconv.shape, F32),
            pltpu.VMEM((DEVICES, LANES, LANES), BF16),
            pltpu.VMEM((DEVICES, 1, LANES), I32),
            pltpu.VMEM((LAT, LANES, LANES), BF16),
            pltpu.VMEM((LAT, DW_ROWS, LANES), BF16),
            pltpu.VMEM((LAT, DW_ROWS, LANES), BF16),
            pltpu.VMEM((LON, 16, LANES), BF16),
            pltpu.VMEM((LON, 16, LANES), BF16),
            pltpu.VMEM((8, LANES), F32),
            pltpu.VMEM((LON, 8, LANES), F32),
            pltpu.VMEM((PART_ROWS, LANES), BF16),
            pltpu.VMEM((LAT, PART_ROWS, LANES), BF16),
            dma((1,)),
            dma((DEVICES // GROUP,)),
            dma((1,)),
            dma((1,)),
            dma((2,)),
            dma((5,)),
            dma((5,)),
            pltpu.SemaphoreType.REGULAR,
        ],
        compiler_params=pltpu.CompilerParams(collective_id=0, has_side_effects=True),
        name="exchange",
    )(rows, cells.reshape(DEVICES, 1, LANES), parts, padded, gconv, table)


def finish_kernel(factor, chunks_ref, grad_ref, up_ref, down_ref, dw_ref, out_ref):
    for chunk in range(LAT):
        block = chunks_ref[chunk].astype(F32) * factor
        if chunk < 4:
            up_ref[:, chunk * LANES : (chunk + 1) * LANES] = block[:LANES]
        else:
            down_ref[(chunk - 4) * LANES : (chunk - 3) * LANES, :] = block[:LANES]
        if chunk < TAPS:
            dw_ref[chunk] = block[LANES : LANES + TAPS]
    out_ref[...] = grad_ref[...]


def finish(chunks, grad, factor):
    return pl.pallas_call(
        functools.partial(finish_kernel, factor),
        out_shape=(
            jax.ShapeDtypeStruct((LANES, 512), F32),
            jax.ShapeDtypeStruct((512, LANES), F32),
            jax.ShapeDtypeStruct((TAPS, TAPS, LANES), F32),
            jax.ShapeDtypeStruct((A_DEV, LANES), F32),
        ),
        in_specs=[VMEM_SPEC] * 2,
        out_specs=[VMEM_SPEC] * 4,
        name="finish",
    )(chunks, grad)


def on_device(
    state,
    forcing,
    cotangent,
    land_mask,
    dw_weight,
    dw_bias,
    norm_gain,
    norm_bias,
    up_weight,
    up_bias,
    down_weight,
    down_bias,
    layer_scale,
    owner,
    atmos_cell,
    weight_index,
    intersection_weights,
):
    rows, cols, channels = state.shape
    padded, slots, cells = exchange_halo(state, owner[:, 0], atmos_cell, weight_index)
    vectors = [
        array.reshape(1, channels)
        for array in (dw_bias, norm_gain, norm_bias, down_bias, layer_scale)
    ]
    result, parts, send_rows, gconv = run_block(
        padded,
        state,
        forcing,
        cotangent,
        land_mask,
        dw_weight,
        vectors,
        up_weight,
        up_bias.reshape(1, -1),
        down_weight,
        slots.reshape(-1),
    )
    factor = float(rows * LAT * cols * LON) ** (-0.5)
    chunks, grad = exchange(send_rows, cells, parts, padded, gconv, intersection_weights)
    grad_up, grad_down, grad_dw, forcing_grad = finish(chunks, grad, factor)
    return (result, grad_dw, grad_up, grad_down, forcing_grad)


def solution(mesh):
    in_specs = (
        P("lat", "lon", None),
        P("lat", "lon", None),
        P("lat", "lon", None),
        P("lat", "lon"),
        P(),
        P(),
        P(),
        P(),
        P(),
        P(),
        P(),
        P(),
        P(),
        P(("lat", "lon"), None),
        P(("lat", "lon")),
        P(("lat", "lon")),
        P(),
    )
    out_specs = (P("lat", "lon", None), P(), P(), P(), P(("lat", "lon"), None))
    return jax.shard_map(
        on_device, mesh=mesh, in_specs=in_specs, out_specs=out_specs, check_vma=False
    )
```
